32 devices in a mesh: wide: 8 (over z, x), grp: 4 (over y, core).
Axes of the slice: x: 2, y: 2, z: 4, core: 2. Of those that a mesh axis runs over, the one named last changes fastest.
Arguments:
- rows_in: bfloat16 [4096, 7168], P('wide', 'grp'), may hold values from -6 to 6
- upstream: bfloat16 [4096, 7168], P('wide', 'grp'), may hold values from -1.5 to 1.5
- probs: float32 [4096], P('wide'), may hold values from 0.05 to 1
- route: int32 [4096, 1], P('wide'), may hold values from 0 to 7; in each aligned block of 512 rows (0 to 511, 512 to 1023, ...) at most 96 rows name the same one
- live: int32 [8], P('wide'), may hold values from 96 to 512, as said below
- gate_up: bfloat16 [8, 7168, 2048], P('wide', 'grp'), may hold values from -0.0625 to 0.0625
- down: bfloat16 [8, 1024, 7168], P('wide', None, 'grp'), may hold values from -0.1875 to 0.1875
Outputs:
- grad_rows: bfloat16 [4096, 7168], P('wide', 'grp')
- grad_prob: bfloat16 [4096], P('wide')
- grad_gate_up: bfloat16 [8, 7168, 2048], P('wide', 'grp')
- grad_down: bfloat16 [8, 1024, 7168], P('wide', None, 'grp')
The draws below stay inside these ranges and needn't reach their ends.
Inputs may be any that keep to these rules, and one draw needn't show every extreme that they name: `route`: in each aligned block of 512 rows no expert is named by more than 96 rows, a bound that some block reaches; every expert is named somewhere. Some block is live in full.
All inputs are finite; a program needn't handle non-finite values.
Results may differ from the reference program's by a relative error of at most 0.01.
Values may be sent and summed in bfloat16 or wider, within the bound.
No kernel may reach another device: no remote copies, remote signals or barrier semaphores. Data moves between devices by JAX's collectives and lax.ppermute only.
A program may use at most 128 MiB of HBM per device.

```python
import math
import jax
import jax.numpy as jnp
import numpy as np
from jax import lax

D = 7168
HIDDEN_SIZE = 1024
ROWS_DEV = 512
EXPERTS = 8
CAP = 96
ROWS = 4096
N_WIDE = 8


def draw_live(key, part):
    rising = ROWS_DEV // 4 + 3 * ROWS_DEV // 4 * jnp.arange(N_WIDE, dtype=jnp.int32) // max(N_WIDE - 1, 1)
    jitter = jax.random.randint(key, (N_WIDE,), 0, ROWS_DEV // 16 + 1)
    jitter = jnp.where(jnp.arange(N_WIDE) == N_WIDE - 1, 0, jitter)
    return (rising - jitter).astype(jnp.int32)


def block_levels(stream_key, shape, pieces, low, largest):
    factor_of, own = 1.0, jax.random.fold_in(stream_key, 6)
    for dim, parts in pieces:
        draws = jnp.exp(jax.random.uniform(jax.random.fold_in(own, dim), (parts,), jnp.float32, low / len(pieces), largest / len(pieces)))
        factor_of = factor_of * jnp.repeat(draws, shape[dim] // parts).reshape([-1 if axis == dim else 1 for axis in range(len(shape))])
    return factor_of


def assign_block(own_key, own, number, rows, number_of, top, most, skew):
    ranking = jax.random.permutation(own_key, number_of)
    packed, common = shares(number_of, rows * top, most, skew, True), shares(number_of, rows * top, most, skew, False)
    places = jnp.arange(number_of)

    def named(lengths, rotation):
        used = int((lengths > 0).sum())
        fixed = max(1, used // 4)
        shifted = fixed + (places - fixed + rotation * (used - fixed)) % max(1, number_of - fixed)
        return jnp.zeros((number_of,), jnp.int32).at[ranking[jnp.where(places < fixed, places, shifted)]].set(jnp.asarray(lengths, jnp.int32))

    lengths = jnp.where(number % 4 == 0, named(packed, number // 4), named(common, number - number // 4 - 1))
    mixed = jax.random.permutation(jax.random.fold_in(own, 3), number_of)
    source_of, taker = mixed[0:number_of // 2 * 2:2], mixed[1:number_of // 2 * 2:2]
    slack = jnp.minimum(lengths[source_of] - 1, most - lengths[taker]) // 2
    slack = jnp.where((source_of == ranking[0]) | (taker == ranking[0]) | (lengths[taker] == 0), 0, jnp.maximum(slack, 0))
    shifted = jax.random.randint(jax.random.fold_in(own, 4), (number_of // 2,), 0, 1 << 20) % (slack + 1)
    lengths = lengths.at[source_of].add(-shifted).at[taker].add(shifted)
    items = jnp.searchsorted(jnp.cumsum(lengths), jnp.arange(rows * top), side="right").astype(jnp.int32)
    table = items.reshape(top, rows).T
    table = table[jax.random.permutation(jax.random.fold_in(own, 1), rows)]
    rotation = jax.random.randint(jax.random.fold_in(own, 2), (rows, 1), 0, top)
    return jnp.take_along_axis(table, (jnp.arange(top)[None, :] + rotation) % top, axis=1)


def shares(amount, total, most, skew, full):
    portions = [(1 << 20) // math.isqrt(rank ** skew) + 1 for rank in range(1, amount + 1)]
    largest = most if full else min(most, max(-(-total // amount), total * portions[0] // sum(portions)))
    least = 1 if total - largest >= amount - 1 else 0
    given, surplus = [largest] + [least] * (amount - 1), total - largest - least * (amount - 1)
    while surplus > 0:
        free = [i for i in range(1, amount) if given[i] < largest] or [i for i in range(1, amount) if given[i] < most]
        mass, remaining = sum([portions[i] for i in free]), surplus
        for i in free:
            more = min(most - given[i], max(1, remaining * portions[i] // mass), surplus)
            given[i] = given[i] + more
            surplus = surplus - more
    return np.array(given)


def noise(key, extent, deviation, limit, pieces=(), kind=jnp.bfloat16):
    drawn = jax.random.normal(key, extent, jnp.float32) * deviation
    if len(pieces) > 0:
        drawn = block_levels(key, extent, pieces, -0.22, 0.18) * drawn
    return jnp.clip(drawn, min=-limit, max=limit).astype(kind)


def setup_inputs(seed: int = 0) -> dict:
    arg_keys = jax.random.split(jax.random.key(seed), 8)
    rows_in = noise(arg_keys[0], (ROWS, D), 1.0, 6.0, ((0, 8), (1, 4)))
    upstream = noise(arg_keys[1], (ROWS, D), 0.25, 1.5, ((0, 8), (1, 4)))
    probs = jnp.clip(jnp.exp(math.log(1.0) - 2.9957323 * jax.random.uniform(arg_keys[2], (ROWS,), jnp.float32) ** block_levels(arg_keys[2], (ROWS,), ((0, 8),), -0.2, 0.2)), 0.05, 1.0)
    route_keys = jax.random.split(jax.random.fold_in(arg_keys[3], 1), ROWS // ROWS_DEV)
    route_turns = jax.random.permutation(jax.random.fold_in(arg_keys[3], 3), ROWS // ROWS_DEV)
    route = jax.vmap(lambda own, number: assign_block(jax.random.fold_in(arg_keys[3], 2), own, number, ROWS_DEV, EXPERTS, 1, CAP, 2))(route_keys, route_turns).reshape((ROWS, 1))
    live = draw_live(jax.random.fold_in(arg_keys[7], 71), 0)
    gate_up = noise(arg_keys[5], (EXPERTS, D, 2 * HIDDEN_SIZE), D ** -0.5, 0.0625, ((0, 8), (1, 4)))
    down = noise(arg_keys[6], (EXPERTS, HIDDEN_SIZE, D), HIDDEN_SIZE ** -0.5, 0.1875, ((0, 8), (2, 4)))
    return {"rows_in": rows_in, "upstream": upstream, "probs": probs, "route": route, "live": live, "gate_up": gate_up, "down": down}


BALANCE = 1.0


def activate(gate, up, grad_hidden):
    sigmoid_gate = jax.nn.sigmoid(gate)
    swish = gate * sigmoid_gate
    hidden = (swish * up).astype(jnp.bfloat16)
    grad_gate = (grad_hidden * up * sigmoid_gate * (1.0 + gate * (1.0 - sigmoid_gate))).astype(jnp.bfloat16)
    grad_up = (grad_hidden * swish).astype(jnp.bfloat16)
    return hidden, grad_gate, grad_up


def reference(rows_in, upstream, probs, route, live, gate_up, down):
    expert_of = route[:, 0].astype(jnp.int32)
    position = jnp.arange(ROWS, dtype=jnp.int32) % ROWS_DEV
    live_bound = jnp.repeat(live.astype(jnp.int32), ROWS_DEV)
    live_mask = (position < live_bound).astype(jnp.float32)
    labels = jnp.arange(EXPERTS, dtype=jnp.int32)
    onehot = (expert_of[:, None] == labels[None, :]).astype(jnp.float32)
    global_loads = jnp.sum(onehot * live_mask[:, None], axis=0)
    load_share = EXPERTS * global_loads / ROWS
    row_share = jnp.sum(onehot * load_share[None, :], axis=1)
    scaled = ((probs * live_mask)[:, None] * upstream.astype(jnp.float32)).astype(jnp.bfloat16)
    totals = jnp.sum(onehot, axis=0).astype(jnp.int32)
    starts = (jnp.cumsum(totals) - totals).astype(jnp.int32)
    row_order = jnp.argsort(expert_of, stable=True).astype(jnp.int32)
    slot_span = N_WIDE * CAP
    offsets = jnp.arange(slot_span, dtype=jnp.int32)
    hidden_width = HIDDEN_SIZE

    def one_expert(expert_index):
        filled = offsets < totals[expert_index]
        picked = row_order[jnp.minimum(starts[expert_index] + offsets, ROWS - 1)].astype(jnp.int32)
        token_rows = rows_in[picked]
        scaled_rows = jnp.where(filled[:, None], scaled[picked], jnp.zeros((), scaled.dtype))
        upward_rows = upstream[picked]
        weight_pair = gate_up[expert_index]
        weight_down = down[expert_index]
        preact = jnp.dot(token_rows, weight_pair, preferred_element_type=jnp.float32)
        grad_hidden = jnp.dot(scaled_rows, weight_down.T, preferred_element_type=jnp.float32)
        hidden, grad_gate, grad_up = activate(preact[:, :hidden_width], preact[:, hidden_width:], grad_hidden)
        grad_pair = jnp.concatenate([grad_gate, grad_up], axis=1)
        grad_local = jnp.dot(grad_pair, weight_pair.T, preferred_element_type=jnp.float32)
        outputs = jnp.dot(hidden, weight_down, preferred_element_type=jnp.float32)
        inner_sum = jnp.sum(outputs * upward_rows.astype(jnp.float32), axis=1)
        pair_grad = jnp.dot(token_rows.T, grad_pair, preferred_element_type=jnp.float32).astype(jnp.bfloat16)
        down_grad = jnp.dot(hidden.T, scaled_rows, preferred_element_type=jnp.float32).astype(jnp.bfloat16)
        grad_local = jnp.where(filled[:, None], grad_local, jnp.zeros((), grad_local.dtype))
        inner_sum = jnp.where(filled, inner_sum, jnp.zeros((), inner_sum.dtype))
        return picked, grad_local, inner_sum, pair_grad, down_grad

    picked, grad_local, inner_sum, pair_grad, down_grad = lax.map(one_expert, labels)
    flat_rows = picked.reshape(-1)
    grad_rows = jnp.zeros((ROWS, D), jnp.float32).at[flat_rows].add(grad_local.reshape(-1, D))
    inner_rows = jnp.zeros((ROWS,), jnp.float32).at[flat_rows].add(inner_sum.reshape(-1))
    inner_rows = inner_rows.astype(jnp.bfloat16).astype(jnp.float32)
    grad_prob = (live_mask * (inner_rows + BALANCE * row_share)).astype(jnp.bfloat16)
    return grad_rows.astype(jnp.bfloat16), grad_prob, pair_grad, down_grad
```

```python
import jax
import jax.numpy as jnp
from jax import lax
from jax.experimental import pallas as pl
from jax.experimental.pallas import tpu as pltpu
from jax.sharding import PartitionSpec as P


BALANCE = 1.0
CHUNKS = 3


def contract_rows(left, right):
    return lax.dot_general(
        left, right, (((0,), (0,)), ((), ())), preferred_element_type=jnp.float32
    )


def contract_last(left, right):
    return lax.dot_general(
        left, right, (((1,), (1,)), ((), ())), preferred_element_type=jnp.float32
    )


def swap(value, axis, members, bits):
    return lax.ppermute(value, axis, [(i, i ^ bits) for i in range(members)])


def halve(parts, index, members):
    bit = 1
    while bit < members:
        upper = (index & bit) != 0
        half = parts[0].shape[1] // 2
        sent = jnp.stack([jnp.where(upper, v[:, :half], v[:, half:]) for v in parts])
        arrived = swap(sent, "grp", members, bit)
        kept = [jnp.where(upper, v[:, half:], v[:, :half]) for v in parts]
        parts = [k.astype(jnp.float32) + a.astype(jnp.float32) for k, a in zip(kept, arrived)]
        bit *= 2
        if bit < members:
            parts = [v.astype(jnp.bfloat16) for v in parts]
    return parts


def double(parts, index, members):
    bit = members // 2
    while bit > 1:
        upper = (index & bit) != 0
        arrived = swap(jnp.stack(parts), "grp", members, bit)
        parts = [
            jnp.concatenate([jnp.where(upper, a, v), jnp.where(upper, v, a)], axis=1)
            for v, a in zip(parts, arrived)
        ]
        bit //= 2
    own = jnp.stack(parts)
    return own, swap(own, "grp", members, bit)


def finish_kernel(index_ref, own_ref, arrived_ref, pair_ref, grad_ref, wide_ref, hidden_ref):
    half = own_ref.shape[2]

    @pl.when(pl.program_id(0) == 0)
    def _():
        upper = (index_ref[0] & 1) != 0
        for kind in range(3):
            target = hidden_ref if kind == 2 else wide_ref
            base = 2 * half * (kind % 2)

            @pl.when(upper)
            def _():
                target[:, base : base + half] = arrived_ref[kind]
                target[:, base + half : base + 2 * half] = own_ref[kind]

            @pl.when(jnp.logical_not(upper))
            def _():
                target[:, base : base + half] = own_ref[kind]
                target[:, base + half : base + 2 * half] = arrived_ref[kind]

    grad_ref[...] = contract_last(wide_ref[...], pair_ref[...]).astype(jnp.bfloat16)


def tile_of(width):
    return 256 if width % 256 == 0 else width


def finish(index, own, arrived, own_pair):
    kinds, rows, half = own.shape
    width = own_pair.shape[0]
    tile = tile_of(width)
    whole = pl.BlockSpec((kinds, rows, half), lambda i, s: (0, 0, 0))
    return pl.pallas_call(
        finish_kernel,
        grid_spec=pltpu.PrefetchScalarGridSpec(
            num_scalar_prefetch=1,
            grid=(width // tile,),
            in_specs=[whole, whole, pl.BlockSpec((tile, 4 * half), lambda i, s: (i, 0))],
            out_specs=[
                pl.BlockSpec((rows, tile), lambda i, s: (0, i)),
                pl.BlockSpec((rows, 4 * half), lambda i, s: (0, 0)),
                pl.BlockSpec((rows, 2 * half), lambda i, s: (0, 0)),
            ],
        ),
        out_shape=[
            jax.ShapeDtypeStruct((rows, width), jnp.bfloat16),
            jax.ShapeDtypeStruct((rows, 4 * half), jnp.bfloat16),
            jax.ShapeDtypeStruct((rows, 2 * half), jnp.bfloat16),
        ],
        cost_estimate=pl.CostEstimate(
            flops=8 * rows * width * half, bytes_accessed=8 * width * half, transcendentals=0
        ),
        name="finish",
    )(index.reshape(1), own, arrived, own_pair)


def weights_kernel(*refs):
    scaled, tokens = refs[:CHUNKS], refs[CHUNKS : 2 * CHUNKS]
    pairs, hiddens = refs[2 * CHUNKS : 3 * CHUNKS], refs[3 * CHUNKS : 4 * CHUNKS]
    pair_ref, down_ref = refs[4 * CHUNKS :]
    pair_total = sum(contract_rows(t[...], p[...]) for t, p in zip(tokens, pairs))
    pair_ref[...] = pair_total.astype(jnp.bfloat16)
    down_total = sum(contract_rows(h[...], v[...]) for h, v in zip(hiddens, scaled))
    down_ref[...] = down_total.astype(jnp.bfloat16)


def weight_grads(arrived, pairs, hiddens, width):
    rows = arrived[0].shape[0]
    hidden_width = hiddens[0].shape[1]
    tile = tile_of(width)
    steps = width // tile
    if steps == 1:
        scaled, tokens, shift = (
            [v[:, :width] for v in arrived],
            [v[:, width:] for v in arrived],
            0,
        )
    else:
        scaled, tokens, shift = arrived, arrived, steps
    return pl.pallas_call(
        weights_kernel,
        grid=(steps,),
        in_specs=[pl.BlockSpec((rows, tile), lambda i: (0, i))] * CHUNKS
        + [pl.BlockSpec((rows, tile), lambda i: (0, i + shift))] * CHUNKS
        + [pl.BlockSpec((rows, 2 * hidden_width), lambda i: (0, 0))] * CHUNKS
        + [pl.BlockSpec((rows, hidden_width), lambda i: (0, 0))] * CHUNKS,
        out_specs=[
            pl.BlockSpec((tile, 2 * hidden_width), lambda i: (i, 0)),
            pl.BlockSpec((hidden_width, tile), lambda i: (0, i)),
        ],
        out_shape=[
            jax.ShapeDtypeStruct((width, 2 * hidden_width), jnp.bfloat16),
            jax.ShapeDtypeStruct((hidden_width, width), jnp.bfloat16),
        ],
        cost_estimate=pl.CostEstimate(
            flops=6 * CHUNKS * rows * width * hidden_width,
            bytes_accessed=6 * width * hidden_width,
            transcendentals=0,
        ),
        name="weight_grads",
    )(*scaled, *tokens, *pairs, *hiddens)


def activate(gate, up, grad_hidden):
    sigmoid_gate = jax.nn.sigmoid(gate)
    swish = gate * sigmoid_gate
    hidden = (swish * up).astype(jnp.bfloat16)
    inner = jnp.sum(hidden.astype(jnp.float32) * grad_hidden, axis=1)
    grad_gate = (grad_hidden * up * sigmoid_gate * (1.0 + gate * (1.0 - sigmoid_gate))).astype(
        jnp.bfloat16
    )
    grad_up = (grad_hidden * swish).astype(jnp.bfloat16)
    return [grad_gate, grad_up, hidden], inner


def exchange(values, experts):
    sent = values.reshape(experts, values.shape[0] // experts, values.shape[1])
    got = lax.all_to_all(sent, "wide", split_axis=0, concat_axis=0, tiled=True)
    return got.reshape(values.shape)


def after(value, *others):
    return lax.optimization_barrier((value, *others))[0]


def on_device(rows_in, upstream, probs, route, live, gate_up, down):
    experts = lax.axis_size("wide")
    members = lax.axis_size("grp")
    index = lax.axis_index("grp")
    rows_dev, width = rows_in.shape
    hidden_width = down.shape[1]
    capacity = rows_dev * 3 // (2 * experts)
    depth = capacity // CHUNKS
    chunk_rows = experts * depth
    own_pair = gate_up[0]
    own_down = down[0]
    expert_of = route[:, 0]
    inside = lax.iota(jnp.int32, rows_dev) < live[0]
    live_mask = inside.astype(jnp.float32)
    labels = lax.iota(jnp.int32, experts)
    onehot = (expert_of[:, None] == labels[None, :]).astype(jnp.int32)
    slot = jnp.sum((jnp.cumsum(onehot, axis=0) - 1) * onehot, axis=1)
    scaled = ((probs * live_mask)[:, None] * upstream.astype(jnp.float32)).astype(jnp.bfloat16)
    both = jnp.concatenate([scaled, rows_in], axis=1)
    target = (slot // depth) * chunk_rows + expert_of * depth + slot % depth

    def arrange(step):
        places = lax.iota(jnp.int32, chunk_rows) + step * chunk_rows
        select = (target[None, :] == places[:, None]).astype(jnp.bfloat16)
        dispatch.append(select)
        return jnp.dot(select, both, preferred_element_type=jnp.float32).astype(jnp.bfloat16)

    def project(block):
        grad_part = contract_last(block[:, :width], own_down).astype(jnp.bfloat16)
        pre_part = jnp.dot(block[:, width:], own_pair, preferred_element_type=jnp.float32)
        pre_part = pre_part.astype(jnp.bfloat16)
        return [pre_part[:, :hidden_width], pre_part[:, hidden_width:], grad_part]

    dispatch, pairs, hiddens, inners = [], [], [], []
    sent = [arrange(step) for step in range(CHUNKS)]
    arrived, parts, returned = [], [], []
    for step in range(CHUNKS):
        if step > 0:
            sent[step] = after(sent[step], arrived[step - 1])
        arrived.append(exchange(sent[step], experts))
        parts.append(project(arrived[step]))
    packed = [None] * CHUNKS
    for step in range(CHUNKS):
        share = halve(parts[step], index, members)
        packed[step], inner = activate(*share)
        inners.append(inner)
    inner_all = jnp.stack(inners, axis=0)
    bit = 1
    while bit < members:
        inner_all = inner_all + swap(inner_all, "grp", members, bit)
        bit *= 2
    local_loads = jnp.sum(onehot * inside.astype(jnp.int32)[:, None], axis=0)
    digits = jnp.concatenate([local_loads // 16, local_loads % 16])
    digits = jnp.broadcast_to(digits.astype(jnp.bfloat16)[None, :], (chunk_rows, 2 * experts))
    extra = jnp.concatenate([inner_all.T.astype(jnp.bfloat16), digits], axis=1)
    extra = jnp.pad(extra, ((0, 0), (0, 128 - extra.shape[1])))
    for step in range(CHUNKS):
        if step == CHUNKS - 1:
            packed[step] = [after(v, returned[0]) for v in packed[step]]
        own, other = double(packed[step], index, members)
        grad_own, grad_pair, hidden = finish(index, own, other, own_pair)
        pairs.append(grad_pair)
        hiddens.append(hidden)
        if step == CHUNKS - 1:
            grad_own = jnp.concatenate([grad_own, extra], axis=1)
        returned.append(exchange(grad_own, experts))

    pair_grad, down_grad = weight_grads(arrived, pairs, hiddens, width)

    tail = returned[-1][:, width:].astype(jnp.float32)
    returned[-1] = returned[-1][:, :width]
    counts = tail.reshape(experts, depth, 128)[:, 0, CHUNKS : CHUNKS + 2 * experts]
    load_share = jnp.sum(counts[:, :experts] * 16 + counts[:, experts:], axis=0) / rows_dev
    hot = (
        (expert_of * depth + slot % depth)[:, None] == lax.iota(jnp.int32, chunk_rows)[None, :]
    ).astype(jnp.float32)
    inner_rows = jnp.zeros((rows_dev,), jnp.float32)
    for step in range(CHUNKS):
        found = jnp.sum(hot * tail[:, step][None, :], axis=1)
        inner_rows = jnp.where(slot // depth == step, found, inner_rows)
    inner_rows = (inner_rows / probs).astype(jnp.bfloat16).astype(jnp.float32)
    row_share = jnp.sum(onehot.astype(jnp.float32) * load_share[None, :], axis=1)
    grad_prob = (live_mask * (inner_rows + BALANCE * row_share)).astype(jnp.bfloat16)

    grad_rows = None
    for step in range(CHUNKS):
        part = contract_rows(dispatch[step], returned[step]).astype(jnp.bfloat16)
        grad_rows = part if grad_rows is None else grad_rows + part
    return grad_rows, grad_prob, pair_grad[None], down_grad[None]


def solution(mesh):
    return jax.shard_map(
        on_device,
        mesh=mesh,
        in_specs=(
            P("wide", "grp"),
            P("wide", "grp"),
            P("wide"),
            P("wide", None),
            P("wide"),
            P("wide", "grp", None),
            P("wide", None, "grp"),
        ),
        out_specs=(P("wide", "grp"), P("wide"), P("wide", "grp", None), P("wide", None, "grp")),
        check_vma=False,
    )
```

```python
import functools

import jax
import jax.numpy as jnp
from jax import lax
from jax.experimental import pallas as pl
from jax.experimental.pallas import tpu as pltpu
from jax.sharding import PartitionSpec as P


BALANCE = 1.0
HIGH, LOW = 64, 96
PARTS = (5, 4, 3)
OUT_DIRECT = (False, True, False)
BACK_DIRECT = (False, False, True)
CHUNKS = len(PARTS)


def contract_rows(left, right):
    return lax.dot_general(
        left, right, (((0,), (0,)), ((), ())), preferred_element_type=jnp.float32
    )


def contract_last(left, right):
    return lax.dot_general(
        left, right, (((1,), (1,)), ((), ())), preferred_element_type=jnp.float32
    )


def swap(value, axis, members, bits):
    return lax.ppermute(value, axis, [(i, i ^ bits) for i in range(members)])


def halve(parts, index, members):
    bit = 1
    first = parts
    while bit < members:
        upper = (index & bit) != 0
        half = parts[0].shape[1] // 2
        sent = jnp.stack([jnp.where(upper, v[:, :half], v[:, half:]) for v in parts])
        arrived = swap(sent, "grp", members, bit)
        kept = [jnp.where(upper, v[:, half:], v[:, :half]) for v in parts]
        parts = [k.astype(jnp.float32) + a.astype(jnp.float32) for k, a in zip(kept, arrived)]
        if bit == 1:
            first = parts
        bit *= 2
        if bit < members:
            parts = [v.astype(jnp.bfloat16) for v in parts]
            first = parts if bit == 2 else first
    return parts, first


def double(parts, index, members):
    bit = members // 2
    while bit > 1:
        upper = (index & bit) != 0
        arrived = swap(jnp.stack(parts), "grp", members, bit)
        parts = [
            jnp.concatenate([jnp.where(upper, a, v), jnp.where(upper, v, a)], axis=1)
            for v, a in zip(parts, arrived)
        ]
        bit //= 2
    own = jnp.stack(parts)
    return own, swap(own, "grp", members, bit)


def finish_kernel(experts, reorder, index_ref, place_ref, *refs):
    own_ref, arrived_ref, pair_ref, extra_ref = refs[:4]
    wide_ref, hidden_ref = refs[4:6]
    outs, held_ref = refs[6:-1], refs[-1]
    half = own_ref.shape[2]
    tile = pair_ref.shape[0]

    @pl.when(pl.program_id(0) == 0)
    def _():
        upper = (index_ref[0] & 1) != 0
        for kind in range(3):
            target = hidden_ref if kind == 2 else wide_ref
            base = 2 * half * (kind % 2)

            @pl.when(upper)
            def _():
                target[:, base : base + half] = arrived_ref[kind]
                target[:, base + half : base + 2 * half] = own_ref[kind]

            @pl.when(jnp.logical_not(upper))
            def _():
                target[:, base : base + half] = own_ref[kind]
                target[:, base + half : base + 2 * half] = arrived_ref[kind]

    grad = contract_last(wide_ref[...], pair_ref[...])
    depth = grad.shape[0] // experts
    if not reorder:
        outs[0][...] = grad.astype(jnp.bfloat16)
        return
    held_ref[...] = grad
    for block in range(experts):
        start = pl.multiple_of((block ^ place_ref[0]) * depth, depth)
        rows = pl.ds(start, depth)
        out = outs[block] if len(outs) > 1 else outs[0].at[block * depth : (block + 1) * depth]
        out[:, :tile] = held_ref[rows, :].astype(jnp.bfloat16)
        if out.shape[1] > tile:
            out[:, tile:] = extra_ref[rows, :].astype(jnp.bfloat16)


def tile_of(width, most):
    tiles = [t for t in range(128, most + 1, 128) if width % t == 0]
    return tiles[-1] if tiles else width


def finish(index, place, own, arrived, own_pair, extra, experts, reorder, split):
    kinds, rows, half = own.shape
    width = own_pair.shape[0]
    tile = width if split else tile_of(width, 1024)
    size = rows // experts if split else rows
    lanes = extra.shape[1] if split else 0
    whole = pl.BlockSpec((kinds, rows, half), lambda i, *_: (0, 0, 0))
    results = pl.pallas_call(
        functools.partial(finish_kernel, experts, reorder),
        grid_spec=pltpu.PrefetchScalarGridSpec(
            num_scalar_prefetch=2,
            grid=(width // tile,),
            in_specs=[
                whole,
                whole,
                pl.BlockSpec((tile, 4 * half), lambda i, *_: (i, 0)),
                pl.BlockSpec(extra.shape, lambda i, *_: (0, 0)),
            ],
            out_specs=[
                pl.BlockSpec((rows, 4 * half), lambda i, *_: (0, 0)),
                pl.BlockSpec((rows, 2 * half), lambda i, *_: (0, 0)),
            ]
            + [pl.BlockSpec((size, tile + lanes), lambda i, *_: (0, i))] * (rows // size),
            scratch_shapes=[pltpu.VMEM((rows, tile), jnp.float32)],
        ),
        out_shape=[
            jax.ShapeDtypeStruct((rows, 4 * half), jnp.bfloat16),
            jax.ShapeDtypeStruct((rows, 2 * half), jnp.bfloat16),
        ]
        + [jax.ShapeDtypeStruct((size, width + lanes), jnp.bfloat16)] * (rows // size),
        cost_estimate=pl.CostEstimate(
            flops=8 * rows * width * half, bytes_accessed=8 * width * half, transcendentals=0
        ),
        name="finish",
    )(index.reshape(1), place.reshape(1), own, arrived, own_pair, extra)
    return results[0], results[1], results[2:]


def weights_kernel(*refs):
    scaled, tokens = refs[:CHUNKS], refs[CHUNKS : 2 * CHUNKS]
    pairs, hiddens = refs[2 * CHUNKS : 3 * CHUNKS], refs[3 * CHUNKS : 4 * CHUNKS]
    pair_ref, down_ref, all_scaled, all_tokens, all_pairs, all_hidden = refs[4 * CHUNKS :]

    def gather(target, sources):
        begin = 0
        for source in sources:
            target[begin : begin + source.shape[0]] = source[...]
            begin += source.shape[0]

    @pl.when(pl.program_id(0) == 0)
    def _():
        gather(all_pairs, pairs)
        gather(all_hidden, hiddens)

    gather(all_tokens, tokens)
    gather(all_scaled, scaled)
    pair_ref[...] = contract_rows(all_tokens[...], all_pairs[...]).astype(jnp.bfloat16)
    down_ref[...] = contract_rows(all_hidden[...], all_scaled[...]).astype(jnp.bfloat16)


def weight_grads(arrived, pairs, hiddens, width):
    rows = [v.shape[0] for v in arrived]
    hidden_width = hiddens[0].shape[1]
    tile = tile_of(width, 1024)
    steps = width // tile
    if steps == 1:
        scaled, tokens, shift = (
            [v[:, :width] for v in arrived],
            [v[:, width:] for v in arrived],
            0,
        )
    else:
        scaled, tokens, shift = arrived, arrived, steps
    return pl.pallas_call(
        weights_kernel,
        grid=(steps,),
        in_specs=[pl.BlockSpec((r, tile), lambda i: (0, i)) for r in rows]
        + [pl.BlockSpec((r, tile), lambda i: (0, i + shift)) for r in rows]
        + [pl.BlockSpec((r, 2 * hidden_width), lambda i: (0, 0)) for r in rows]
        + [pl.BlockSpec((r, hidden_width), lambda i: (0, 0)) for r in rows],
        out_specs=[
            pl.BlockSpec((tile, 2 * hidden_width), lambda i: (i, 0)),
            pl.BlockSpec((hidden_width, tile), lambda i: (0, i)),
        ],
        out_shape=[
            jax.ShapeDtypeStruct((width, 2 * hidden_width), jnp.bfloat16),
            jax.ShapeDtypeStruct((hidden_width, width), jnp.bfloat16),
        ],
        scratch_shapes=[
            pltpu.VMEM((sum(rows), tile), jnp.bfloat16),
            pltpu.VMEM((sum(rows), tile), jnp.bfloat16),
            pltpu.VMEM((sum(rows), 2 * hidden_width), jnp.bfloat16),
            pltpu.VMEM((sum(rows), hidden_width), jnp.bfloat16),
        ],
        cost_estimate=pl.CostEstimate(
            flops=6 * sum(rows) * width * hidden_width,
            bytes_accessed=6 * width * hidden_width,
            transcendentals=0,
        ),
        name="weight_grads",
    )(*scaled, *tokens, *pairs, *hiddens)


def activate(gate, up, grad_hidden):
    sigmoid_gate = jax.nn.sigmoid(gate)
    swish = gate * sigmoid_gate
    hidden = (swish * up).astype(jnp.bfloat16)
    inner = jnp.sum(hidden.astype(jnp.float32) * grad_hidden, axis=1)
    grad_gate = (grad_hidden * up * sigmoid_gate * (1.0 + gate * (1.0 - sigmoid_gate))).astype(
        jnp.bfloat16
    )
    grad_up = (grad_hidden * swish).astype(jnp.bfloat16)
    return [grad_gate, grad_up, hidden], inner


def exchange(values, experts):
    sent = values.reshape(experts, values.shape[0] // experts, values.shape[1])
    got = lax.all_to_all(sent, "wide", split_axis=0, concat_axis=0, tiled=True)
    return got.reshape(values.shape)


def join_kernel(*refs):
    out_ref = refs[-1]
    depth = refs[0].shape[0]
    for s, piece in enumerate(refs[:-1]):
        out_ref[s * depth : (s + 1) * depth] = piece[...]


def join(pieces):
    depth, width = pieces[0].shape
    tile = tile_of(width, 1024)
    return pl.pallas_call(
        join_kernel,
        grid=(width // tile,),
        in_specs=[pl.BlockSpec((depth, tile), lambda i: (0, i))] * len(pieces),
        out_specs=pl.BlockSpec((len(pieces) * depth, tile), lambda i: (0, i)),
        out_shape=jax.ShapeDtypeStruct((len(pieces) * depth, width), jnp.bfloat16),
        name="join",
    )(*pieces)


def exchange_direct(pieces, experts):
    got = [None] * experts
    for s in reversed(range(experts)):
        got[s] = pieces[s] if s == 0 else swap(pieces[s], "wide", experts, s)
    return got


def arrange_kernel(experts, begin, depth, direct, live_ref, place_ref, *refs):
    route_ref, probs_ref, upstream_ref, rows_ref = refs[:4]
    outs, slot_ref, select_ref, factor_ref = refs[4:-3], refs[-3], refs[-2], refs[-1]
    count = experts * depth
    step = pl.program_id(0)
    rows_dev = route_ref.shape[1]

    @pl.when(step == 0)
    def _():
        expert = route_ref[...]
        labels = lax.broadcasted_iota(jnp.int32, (experts, rows_dev), 0)
        onehot = (labels == expert).astype(jnp.float32)
        before = lax.broadcasted_iota(jnp.int32, (rows_dev, rows_dev), 0)
        here = lax.broadcasted_iota(jnp.int32, (rows_dev, rows_dev), 1)
        earlier = (before < here).astype(jnp.bfloat16)
        ranks = jnp.dot(
            onehot.astype(jnp.bfloat16), earlier, preferred_element_type=jnp.float32
        )
        slot = jnp.sum(onehot * ranks, axis=0, keepdims=True).astype(jnp.int32)
        slot_ref[...] = slot
        block = expert ^ place_ref[0] if direct else expert
        local = slot - begin
        target = jnp.where((local >= 0) & (local < depth), block * depth + local, -1)
        places = lax.broadcasted_iota(jnp.int32, (count, rows_dev), 0)
        select = (places == target).astype(jnp.float32)
        select_ref[...] = select.astype(jnp.bfloat16)
        inside = lax.broadcasted_iota(jnp.int32, (1, rows_dev), 1) < live_ref[0]
        factor = jnp.where(inside, probs_ref[...], 0.0)
        factor_ref[...] = jnp.sum(select * factor, axis=1, keepdims=True)

    def put(value):
        value = value.astype(jnp.bfloat16)
        if len(outs) == 1:
            outs[0][...] = value
        else:
            for s, out in enumerate(outs):
                out[...] = value[s * depth : (s + 1) * depth]

    half = pl.num_programs(0) // 2

    @pl.when(step < half)
    def _():
        picked = jnp.dot(select_ref[...], upstream_ref[...], preferred_element_type=jnp.float32)
        put(picked * factor_ref[...])

    @pl.when(step >= half)
    def _():
        put(jnp.dot(select_ref[...], rows_ref[...], preferred_element_type=jnp.float32))


def arrange(live, place, route, probs, upstream, rows_in, experts, begin, depth, direct):
    rows_dev, width = upstream.shape
    tile = tile_of(width, 1024)
    half = width // tile
    count = experts * depth
    row = pl.BlockSpec((1, rows_dev), lambda i, *_: (0, 0))
    split = [depth] * experts if direct else [count]
    lanes = -(-width // 128) * 128
    padded = lanes != width
    results = pl.pallas_call(
        functools.partial(arrange_kernel, experts, begin, depth, direct),
        grid_spec=pltpu.PrefetchScalarGridSpec(
            num_scalar_prefetch=2,
            grid=(2 * half,),
            in_specs=[
                row,
                row,
                pl.BlockSpec((rows_dev, tile), lambda i, *_: (0, jnp.minimum(i, half - 1))),
                pl.BlockSpec((rows_dev, tile), lambda i, *_: (0, jnp.maximum(i - half, 0))),
            ],
            out_specs=[
                pl.BlockSpec((None, size, tile), lambda i, *_: (i // half, 0, i % half))
                if padded
                else pl.BlockSpec((size, tile), lambda i, *_: (0, i))
                for size in split
            ]
            + [row],
            scratch_shapes=[
                pltpu.VMEM((count, rows_dev), jnp.bfloat16),
                pltpu.VMEM((count, 1), jnp.float32),
            ],
        ),
        out_shape=[
            jax.ShapeDtypeStruct((2, size, width) if padded else (size, 2 * width), jnp.bfloat16)
            for size in split
        ]
        + [jax.ShapeDtypeStruct((1, rows_dev), jnp.int32)],
        cost_estimate=pl.CostEstimate(
            flops=4 * count * rows_dev * width,
            bytes_accessed=4 * rows_dev * width,
            transcendentals=0,
        ),
        name="arrange",
    )(live, place, route, probs, upstream, rows_in)
    pieces = results[:-1]
    if padded:
        pieces = [jnp.concatenate([v[0], v[1]], axis=1) for v in pieces]
    return pieces, results[-1][0]


def after(value, *others):
    return lax.optimization_barrier((value, *others))[0]


def collect_kernel(experts, per_row, live_ref, place_ref, *refs):
    route_ref, slot_ref, probs_ref, partial_ref = refs[:4]
    pieces, extras = refs[4 : 4 + experts], refs[4 + experts : 4 + 2 * experts]
    rows_ref, prob_ref, select_ref, held_ref, extra_ref = refs[4 + 2 * experts :]
    depth = pieces[0].shape[0]
    count = experts * depth
    rows_dev = route_ref.shape[1]
    begin = per_row * depth - depth

    @pl.when(pl.program_id(0) == 0)
    def _():
        expert, slot = route_ref[...], slot_ref[...]
        block = expert ^ place_ref[0]
        local = slot - begin
        target = jnp.where(local >= 0, block * depth + local, -1)
        places = lax.broadcasted_iota(jnp.int32, (count, rows_dev), 0)
        select_ref[...] = (places == target).astype(jnp.float32).astype(jnp.bfloat16)
        for s in range(experts):
            extra_ref[s * depth : (s + 1) * depth] = extras[s][...].astype(jnp.float32)
        extra = extra_ref[...].astype(jnp.bfloat16)
        source = block * depth + slot // per_row
        chosen = (places == source).astype(jnp.float32).astype(jnp.bfloat16)
        found = contract_rows(extra, chosen)
        lanes = lax.broadcasted_iota(jnp.int32, found.shape, 0)
        inner = jnp.sum(
            jnp.where(lanes == slot % per_row, found, 0.0), axis=0, keepdims=True
        )
        inner = (inner / probs_ref[...]).astype(jnp.bfloat16).astype(jnp.float32)
        heads = (lax.broadcasted_iota(jnp.int32, (count, rows_dev), 0) % depth == 0).astype(
            jnp.float32
        )
        counts = contract_rows(extra, heads.astype(jnp.bfloat16))
        share = jnp.sum(
            jnp.where(lanes == HIGH + expert, 16.0 * counts, 0.0)
            + jnp.where(lanes == LOW + expert, counts, 0.0),
            axis=0,
            keepdims=True,
        )
        inside = lax.broadcasted_iota(jnp.int32, (1, rows_dev), 1) < live_ref[0]
        total = jnp.where(inside, inner + BALANCE * (share / rows_dev), 0.0)
        prob_ref[...] = total.astype(jnp.bfloat16)

    for s in range(experts):
        held_ref[s * depth : (s + 1) * depth] = pieces[s][...].astype(jnp.float32)
    part = contract_rows(select_ref[...], held_ref[...].astype(jnp.bfloat16))
    rows_ref[...] = (part + partial_ref[...].astype(jnp.float32)).astype(jnp.bfloat16)


def collect(live, place, route, slot, probs, partial, pieces, per_row):
    rows_dev, width = partial.shape
    experts = len(pieces)
    depth, _ = pieces[0].shape
    if width % 128 == 0:
        tile, mains, shift = tile_of(width, 1024), pieces, width // 128
    else:
        tile, mains, shift = width, [v[:, :width] for v in pieces], 0
        pieces = [v[:, width:] for v in pieces]
    row = pl.BlockSpec((1, rows_dev), lambda i, *_: (0, 0))
    count = experts * depth
    return pl.pallas_call(
        functools.partial(collect_kernel, experts, per_row),
        grid_spec=pltpu.PrefetchScalarGridSpec(
            num_scalar_prefetch=2,
            grid=(width // tile,),
            in_specs=[row, row, row, pl.BlockSpec((rows_dev, tile), lambda i, *_: (0, i))]
            + [pl.BlockSpec((depth, tile), lambda i, *_: (0, i))] * experts
            + [pl.BlockSpec((depth, 128), lambda i, *_: (0, shift))] * experts,
            out_specs=[pl.BlockSpec((rows_dev, tile), lambda i, *_: (0, i)), row],
            scratch_shapes=[
                pltpu.VMEM((count, rows_dev), jnp.bfloat16),
                pltpu.VMEM((count, tile), jnp.float32),
                pltpu.VMEM((count, 128), jnp.float32),
            ],
        ),
        out_shape=[
            jax.ShapeDtypeStruct((rows_dev, width), jnp.bfloat16),
            jax.ShapeDtypeStruct((1, rows_dev), jnp.bfloat16),
        ],
        name="collect",
    )(live, place, route, slot, probs, partial, *mains, *pieces)


def on_device(rows_in, upstream, probs, route, live, gate_up, down):
    experts = lax.axis_size("wide")
    members = lax.axis_size("grp")
    index = lax.axis_index("grp")
    place = lax.axis_index("wide")
    rows_dev, width = rows_in.shape
    hidden_width = down.shape[1]
    capacity = rows_dev * 3 // (2 * experts)
    depths = [capacity * part // sum(PARTS) // 8 * 8 for part in PARTS]
    depths[0] += capacity - sum(depths)
    begins = [sum(depths[:step]) for step in range(CHUNKS)]
    own_pair = gate_up[0]
    own_down = down[0]
    expert_of = route[:, 0]
    inside = lax.iota(jnp.int32, rows_dev) < live[0]
    live_mask = inside.astype(jnp.float32)
    labels = lax.iota(jnp.int32, experts)
    onehot = (expert_of[:, None] == labels[None, :]).astype(jnp.int32)
    flat = (live, place.reshape(1), route.reshape(1, rows_dev), probs.reshape(1, rows_dev))
    sent = []
    for step in range(CHUNKS):
        pieces, slots = arrange(
            *flat, upstream, rows_in, experts, begins[step], depths[step], OUT_DIRECT[step]
        )
        sent.append(pieces)
        slot = slots if step == 0 else slot

    def selector(step):
        block = expert_of ^ place if BACK_DIRECT[step] else expert_of
        local = slot - begins[step]
        held = (local >= 0) & (local < depths[step])
        target = jnp.where(held, block * depths[step] + local, -1)
        places = lax.iota(jnp.int32, experts * depths[step])
        return (target[None, :] == places[:, None]).astype(jnp.bfloat16)

    def project(block):
        grad_part = contract_last(block[:, :width], own_down).astype(jnp.bfloat16)
        pre_part = jnp.dot(block[:, width:], own_pair, preferred_element_type=jnp.float32)
        pre_part = pre_part.astype(jnp.bfloat16)
        return [pre_part[:, :hidden_width], pre_part[:, hidden_width:], grad_part]

    pairs, hiddens, inners = [], [], []
    arrived, parts, returned = [], [], []
    packed = []

    def receive(step):
        if OUT_DIRECT[step]:
            arrived.append(join(exchange_direct(sent[step], experts)))
        else:
            arrived.append(exchange(sent[step][0], experts))

    def process(step):
        parts.append(project(arrived[step]))
        share, _ = halve(parts[step], index, members)
        values, inner = activate(*share)
        packed.append(values)
        inner = inner.reshape(experts, depths[step])
        inners.append(inner[labels ^ place] if OUT_DIRECT[step] else inner)

    receive(0)
    sent[1] = [after(v, arrived[0]) for v in sent[1]]
    receive(1)
    process(0)
    sent[2] = [after(v, *packed[0]) for v in sent[2]]
    receive(2)
    process(1)
    process(2)
    inner_all = jnp.concatenate(inners, axis=1)
    bit = 1
    while bit < members:
        inner_all = inner_all + swap(inner_all, "grp", members, bit)
        bit *= 2
    local_loads = jnp.sum(onehot * inside.astype(jnp.int32)[:, None], axis=0)
    digits = jnp.concatenate([local_loads // 16, local_loads % 16]).astype(jnp.float32)
    last_rows = experts * depths[-1]
    per_row = capacity // depths[-1]
    blank = jnp.zeros((HIGH - per_row,), jnp.float32)
    gap = jnp.zeros((LOW - HIGH - experts,), jnp.float32)
    rest = jnp.zeros((128 - LOW - experts,), jnp.float32)
    digits = jnp.concatenate([blank, digits[:experts], gap, digits[experts:], rest])
    digits = jnp.broadcast_to(digits[None, :], (last_rows, 128 - per_row))
    extra = jnp.concatenate([inner_all.reshape(last_rows, per_row), digits], axis=1)
    for step in range(CHUNKS):
        own, other = double(packed[step], index, members)
        grad_pair, hidden, outs = finish(
            index,
            place,
            own,
            other,
            own_pair,
            extra if step == CHUNKS - 1 else jnp.zeros((8, 128), jnp.float32),
            experts,
            OUT_DIRECT[step] != BACK_DIRECT[step],
            step == CHUNKS - 1,
        )
        pairs.append(grad_pair)
        hiddens.append(hidden)
        if step == 0:
            outs = [after(outs[0], arrived[-1])]
        if step == 1:
            outs = [after(outs[0], returned[0], *packed[2])]
        if BACK_DIRECT[step]:
            returned.append(exchange_direct(outs, experts))
        else:
            returned.append(exchange(outs[0], experts))

    pair_grad, down_grad = weight_grads(arrived, pairs, hiddens, width)

    partial = None
    for step in range(CHUNKS - 1):
        part = contract_rows(selector(step), returned[step]).astype(jnp.bfloat16)
        partial = part if partial is None else partial + part
    grad_rows, grad_prob = collect(
        flat[0], flat[1], flat[2], slot[None, :], flat[3], partial, returned[-1], per_row
    )
    grad_prob = grad_prob[0]
    return grad_rows, grad_prob, pair_grad[None], down_grad[None]


def solution(mesh):
    return jax.shard_map(
        on_device,
        mesh=mesh,
        in_specs=(
            P("wide", "grp"),
            P("wide", "grp"),
            P("wide"),
            P("wide", None),
            P("wide"),
            P("wide", "grp", None),
            P("wide", None, "grp"),
        ),
        out_specs=(P("wide", "grp"), P("wide"), P("wide", "grp", None), P("wide", None, "grp")),
        check_vma=False,
    )
```
